128 devices in a mesh: ctx: 16 (over x_hi, z, core), head: 8 (over x_lo, y).
Axes of the slice: x: 4 (x_hi: 2, x_lo: 2; x = x_hi * 2 + x_lo), y: 4, z: 4, core: 2. Of those that a mesh axis runs over, the one named last changes fastest.
Arguments:
- queries: bfloat16 [2, 24576, 4096], P(None, 'ctx', 'head')
- layer_keys_input: bfloat16 [2, 24576, 2048], P(None, 'ctx', 'head')
- layer_values_input: bfloat16 [2, 24576, 2048], P(None, 'ctx', 'head')
- attn_out: bfloat16 [2, 24576, 4096], P(None, 'ctx', 'head'), as said below
- grad_out: bfloat16 [2, 24576, 4096], P(None, 'ctx', 'head'), may hold values from -6 to 6
- log_norm: float32 [2, 32, 24576], P(None, 'head', 'ctx'), as said below
- window: int32 [2], replicated, may hold values from 512 to 1024, as said below
Outputs:
- grad_query: bfloat16 [2, 24576, 4096], P(None, ('ctx', 'head'))
- grad_key: bfloat16 [2, 24576, 2048], P(None, ('ctx', 'head'))
- grad_value: bfloat16 [2, 24576, 2048], P(None, ('ctx', 'head'))
The draws below stay inside these ranges and needn't reach their ends.
Inputs may be any that keep to these rules, and one draw needn't show every extreme that they name: Each layer's window is 512 to 1024 tokens; one of the layers has exactly 1024. log_norm is the log of the sum, over each query's window, of exp of its scaled scores against layer_keys_input. attn_out is the attention output that these weights give from layer_values_input.
All inputs are finite; a program needn't handle non-finite values.
Results may differ from the reference program's by a relative error of at most 0.005.
Values may be sent and summed in bfloat16 or wider, within the bound.
A program may use at most 256 MiB of HBM per device.

```python
import jax
import jax.numpy as jnp
from jax import lax

QUERY_HEADS = 32
KEY_VALUE_HEADS = 16
HEAD_SIZE = 128
WINDOW_LENGTH = 1024
QUERY_PRE = 168
SLIDING_LAYERS = 2
BLOCK = 512
SPAN_TOKENS = 24576


def shared_draws(key):
    which_layer = jax.random.randint(jax.random.fold_in(key, 11), (), 0, SLIDING_LAYERS)
    other_width = jax.random.randint(jax.random.fold_in(key, 12), (SLIDING_LAYERS,), WINDOW_LENGTH // 2, WINDOW_LENGTH + 1)
    widths = jnp.where(jnp.arange(SLIDING_LAYERS) == which_layer, WINDOW_LENGTH, other_width).astype(jnp.int32)
    q_shape = (SLIDING_LAYERS, SPAN_TOKENS, QUERY_HEADS * HEAD_SIZE)
    key_value_shape = (SLIDING_LAYERS, SPAN_TOKENS, KEY_VALUE_HEADS * HEAD_SIZE)
    q_draw = jax.random.normal(jax.random.fold_in(key, 13), q_shape, jnp.float32)
    k_draw = jax.random.normal(jax.random.fold_in(key, 14), key_value_shape, jnp.float32)
    v_draw = jax.random.normal(jax.random.fold_in(key, 15), key_value_shape, jnp.float32)
    return (widths, q_draw.astype(jnp.bfloat16), k_draw.astype(jnp.bfloat16), v_draw.astype(jnp.bfloat16))


def forward_layer(layer_query_rows, layer_key_rows, layer_value_rows, win):
    query_group_count = QUERY_HEADS // KEY_VALUE_HEADS
    score_scale = QUERY_PRE ** (-0.5)
    query_head_count = layer_query_rows.astype(jnp.float32).reshape(SPAN_TOKENS, KEY_VALUE_HEADS, query_group_count, HEAD_SIZE)
    padding_rows = jnp.zeros((WINDOW_LENGTH, KEY_VALUE_HEADS, HEAD_SIZE), jnp.float32)
    padded_keys = jnp.concatenate([padding_rows, layer_key_rows.astype(jnp.float32).reshape(SPAN_TOKENS, KEY_VALUE_HEADS, HEAD_SIZE)], 0)
    padded_values = jnp.concatenate([padding_rows, layer_value_rows.astype(jnp.float32).reshape(SPAN_TOKENS, KEY_VALUE_HEADS, HEAD_SIZE)], 0)

    def one_block(block_idx):
        start_row = block_idx * BLOCK
        q_block = lax.dynamic_slice_in_dim(query_head_count, start_row, BLOCK, 0)
        k_block = lax.dynamic_slice_in_dim(padded_keys, start_row, WINDOW_LENGTH + BLOCK, 0)
        v_block = lax.dynamic_slice_in_dim(padded_values, start_row, WINDOW_LENGTH + BLOCK, 0)
        scores = jnp.einsum('rkgd,ckd->kgrc', q_block, k_block) * score_scale
        q_pos = start_row + jnp.arange(BLOCK, dtype=jnp.int32)
        k_pos = start_row - WINDOW_LENGTH + jnp.arange(WINDOW_LENGTH + BLOCK, dtype=jnp.int32)
        visible = (k_pos[None, :] <= q_pos[:, None]) & (q_pos[:, None] - k_pos[None, :] < win) & (k_pos[None, :] >= 0)
        masked = jnp.where(visible, scores, -1e+30)
        top_score = jnp.max(masked, axis=-1, keepdims=True)
        weights = jnp.where(visible, jnp.exp(masked - top_score), 0.0)
        totals = jnp.sum(weights, axis=-1)
        lse_block = top_score[..., 0] + jnp.log(totals)
        out_block = jnp.einsum('kgrc,ckd->rkgd', weights, v_block) / jnp.transpose(totals, (2, 0, 1))[..., None]
        return (out_block.reshape(BLOCK, QUERY_HEADS * HEAD_SIZE), lse_block.reshape(QUERY_HEADS, BLOCK))
    out_blocks, lse_blocks = lax.map(one_block, jnp.arange(SPAN_TOKENS // BLOCK, dtype=jnp.int32))
    return (out_blocks.reshape(SPAN_TOKENS, QUERY_HEADS * HEAD_SIZE), jnp.transpose(lse_blocks, (1, 0, 2)).reshape(QUERY_HEADS, SPAN_TOKENS))


def forward_all(key):
    widths, q_all, k_all, v_all = shared_draws(key)
    out_list = []
    lse_list = []
    for layer_number in range(SLIDING_LAYERS):
        out_layer, lse_layer = forward_layer(q_all[layer_number], k_all[layer_number], v_all[layer_number], widths[layer_number])
        out_list.append(out_layer)
        lse_list.append(lse_layer)
    return (jnp.stack(out_list, 0), jnp.stack(lse_list, 0))


def draw_window(key, part):
    return shared_draws(key)[0]


def draw_queries(key, part):
    return shared_draws(key)[1]


def draw_layer_keys_input(key, part):
    return shared_draws(key)[2]


def draw_layer_values_input(key, part):
    return shared_draws(key)[3]


def draw_attn_out(key, part):
    return forward_all(key)[0].astype(jnp.bfloat16)


def draw_log_norm(key, part):
    return forward_all(key)[1].astype(jnp.float32)


def block_scale(key, shape, shards, low, high):
    level = 1.0
    for dim, blocks in shards:
        heights = jax.random.uniform(jax.random.fold_in(jax.random.fold_in(key, 6), dim), (blocks,), jnp.float32, low / len(shards), high / len(shards))
        level = level * jnp.repeat(jnp.exp(heights), shape[dim] // blocks).reshape((-1,) + (1,) * (len(shape) - 1 - dim))
    return level


def scatter_about(key, shape, width, most, split=(), kind=jnp.bfloat16):
    values = jax.random.normal(key, shape, jnp.float32) * width
    if len(split) > 0:
        values = block_scale(key, shape, split, -0.22, 0.18) * values
    return jnp.clip(values, min=-most, max=most).astype(kind)


def setup_inputs(seed: int = 0) -> dict:
    key_list = jax.random.split(jax.random.key(seed), 8)
    return {
        "queries": draw_queries(jax.random.fold_in(key_list[7], 71), 0),
        "layer_keys_input": draw_layer_keys_input(jax.random.fold_in(key_list[7], 71), 0),
        "layer_values_input": draw_layer_values_input(jax.random.fold_in(key_list[7], 71), 0),
        "attn_out": draw_attn_out(jax.random.fold_in(key_list[7], 71), 0),
        "grad_out": scatter_about(key_list[4], (SLIDING_LAYERS, SPAN_TOKENS, QUERY_HEADS * HEAD_SIZE), 1.0, 6.0, ((1, 16), (2, 8))),
        "log_norm": draw_log_norm(jax.random.fold_in(key_list[7], 71), 0),
        "window": draw_window(jax.random.fold_in(key_list[7], 71), 0),
    }


def block_grads(q_block, do_block, lse_block, dlt_block, k_block, v_block, q_pos, k_pos, win):
    row_count, head_count, head_dim = q_block.shape
    kv_count = k_block.shape[1]
    query_group_count = head_count // kv_count
    score_scale = QUERY_PRE ** -0.5
    query_head_count = q_block.reshape(row_count, kv_count, query_group_count, head_dim).astype(jnp.float32)
    do_heads = do_block.reshape(row_count, kv_count, query_group_count, head_dim).astype(jnp.float32)
    k_float = k_block.astype(jnp.float32)
    v_float = v_block.astype(jnp.float32)
    scores = jnp.einsum("rkgd,ckd->kgrc", query_head_count, k_float) * score_scale
    lse_heads = lse_block.reshape(kv_count, query_group_count, row_count)
    dlt_heads = dlt_block.reshape(kv_count, query_group_count, row_count)
    visible = (k_pos[None, :] <= q_pos[:, None]) & (q_pos[:, None] - k_pos[None, :] < win) & (k_pos[None, :] >= 0)
    attn_prob = jnp.where(visible, jnp.exp(scores - lse_heads[..., None]), 0.0)
    prob_low = lax.optimization_barrier(attn_prob.astype(jnp.bfloat16)).astype(jnp.float32)
    grad_prob = jnp.einsum("rkgd,ckd->kgrc", do_heads, v_float)
    grad_score = attn_prob * (grad_prob - dlt_heads[..., None])
    score_low = lax.optimization_barrier(grad_score.astype(jnp.bfloat16)).astype(jnp.float32)
    dv_part = jnp.einsum("kgrc,rkgd->ckd", prob_low, do_heads)
    dk_part = jnp.einsum("kgrc,rkgd->ckd", score_low, query_head_count) * score_scale
    dq_part = jnp.einsum("kgrc,ckd->rkgd", score_low, k_float) * score_scale
    return dq_part.reshape(row_count, head_count, head_dim), dk_part, dv_part


def reference(queries, layer_keys_input, layer_values_input, attn_out, grad_out, log_norm, window):
    dq_list = []
    key_gradient_parts = []
    value_gradient_parts = []
    for layer_number in range(SLIDING_LAYERS):
        q_all = queries[layer_number].reshape(SPAN_TOKENS, QUERY_HEADS, HEAD_SIZE)
        do_all = grad_out[layer_number].reshape(SPAN_TOKENS, QUERY_HEADS, HEAD_SIZE)
        delta = jnp.sum(do_all.astype(jnp.float32) * attn_out[layer_number].reshape(SPAN_TOKENS, QUERY_HEADS, HEAD_SIZE).astype(jnp.float32), axis=-1).T
        padding_rows = jnp.zeros((WINDOW_LENGTH, KEY_VALUE_HEADS, HEAD_SIZE), layer_keys_input.dtype)
        padded_keys = jnp.concatenate([padding_rows, layer_keys_input[layer_number].reshape(SPAN_TOKENS, KEY_VALUE_HEADS, HEAD_SIZE)], 0)
        padded_values = jnp.concatenate([padding_rows, layer_values_input[layer_number].reshape(SPAN_TOKENS, KEY_VALUE_HEADS, HEAD_SIZE)], 0)
        win = window[layer_number]
        lse_all = log_norm[layer_number]

        def sweep(block_idx, carry, q_all=q_all, do_all=do_all, delta=delta, padded_keys=padded_keys, padded_values=padded_values, win=win, lse_all=lse_all):
            dq_all, key_gradient_total, value_gradient_total = carry
            start_row = (block_idx * BLOCK).astype(jnp.int32)
            q_block = lax.dynamic_slice_in_dim(q_all, start_row, BLOCK, 0)
            do_block = lax.dynamic_slice_in_dim(do_all, start_row, BLOCK, 0)
            lse_block = lax.dynamic_slice_in_dim(lse_all, start_row, BLOCK, 1)
            dlt_block = lax.dynamic_slice_in_dim(delta, start_row, BLOCK, 1)
            k_block = lax.dynamic_slice_in_dim(padded_keys, start_row, WINDOW_LENGTH + BLOCK, 0)
            v_block = lax.dynamic_slice_in_dim(padded_values, start_row, WINDOW_LENGTH + BLOCK, 0)
            q_pos = start_row + jnp.arange(BLOCK, dtype=jnp.int32)
            k_pos = start_row - WINDOW_LENGTH + jnp.arange(WINDOW_LENGTH + BLOCK, dtype=jnp.int32)
            dq_part, dk_part, dv_part = block_grads(q_block, do_block, lse_block, dlt_block, k_block, v_block, q_pos, k_pos, win)
            dq_all = lax.dynamic_update_slice_in_dim(dq_all, dq_part.astype(jnp.bfloat16), start_row, 0)
            dk_old = lax.dynamic_slice_in_dim(key_gradient_total, start_row, WINDOW_LENGTH + BLOCK, 0)
            dv_old = lax.dynamic_slice_in_dim(value_gradient_total, start_row, WINDOW_LENGTH + BLOCK, 0)
            key_gradient_total = lax.dynamic_update_slice_in_dim(key_gradient_total, dk_old + dk_part, start_row, 0)
            value_gradient_total = lax.dynamic_update_slice_in_dim(value_gradient_total, dv_old + dv_part, start_row, 0)
            return dq_all, key_gradient_total, value_gradient_total

        initial_state = (jnp.zeros((SPAN_TOKENS, QUERY_HEADS, HEAD_SIZE), jnp.bfloat16), jnp.zeros((WINDOW_LENGTH + SPAN_TOKENS, KEY_VALUE_HEADS, HEAD_SIZE), jnp.float32), jnp.zeros((WINDOW_LENGTH + SPAN_TOKENS, KEY_VALUE_HEADS, HEAD_SIZE), jnp.float32))
        dq_all, key_gradient_total, value_gradient_total = lax.fori_loop(0, SPAN_TOKENS // BLOCK, sweep, initial_state)
        dq_list.append(dq_all.reshape(SPAN_TOKENS, QUERY_HEADS * HEAD_SIZE))
        key_gradient_parts.append(key_gradient_total[WINDOW_LENGTH:].astype(jnp.bfloat16).reshape(SPAN_TOKENS, KEY_VALUE_HEADS * HEAD_SIZE))
        value_gradient_parts.append(value_gradient_total[WINDOW_LENGTH:].astype(jnp.bfloat16).reshape(SPAN_TOKENS, KEY_VALUE_HEADS * HEAD_SIZE))
    return jnp.stack(dq_list, 0), jnp.stack(key_gradient_parts, 0), jnp.stack(value_gradient_parts, 0)
```

```python
import functools
import math

import jax
import jax.numpy as jnp
from jax import lax
from jax.experimental import pallas as pl
from jax.experimental.pallas import tpu as pltpu
from jax.sharding import PartitionSpec as P

HEAD_SIZE = 128
WINDOW_LENGTH = 1024
QUERY_PRE = 168
SLIDING_LAYERS = 2
ROWS = 128
SCALE = QUERY_PRE ** (-0.5)
LOG2_E = math.log2(math.e)
HIDDEN = -1e30
MESH = pl.DeviceIdType.MESH
BIASED = (0, 4, 5, 6, 7, 8)
NT = (((1,), (1,)), ((), ()))
NN = (((1,), (0,)), ((), ()))


def dot(a, b, dims=NN):
    return lax.dot_general(a, b, dims, preferred_element_type=jnp.float32)


def kernel(
    head_count,
    ctx_count,
    win_ref,
    lse_ref,
    q_hbm,
    k_hbm,
    v_hbm,
    o_hbm,
    g_hbm,
    dq_out,
    dk_out,
    dv_out,
    q_all,
    g_all,
    o_all,
    k_ext,
    v_ext,
    k_turned,
    bias,
    prob_buf,
    score_buf,
    dk_acc,
    dv_acc,
    dq_stage,
    dk_stage,
    dv_stage,
    back_send,
    back_recv,
    load_sem,
    rim_send_sem,
    rim_recv_sem,
    back_send_sem,
    back_recv_sem,
    out_send_sem,
    out_recv_sem,
    own_sem,
):
    ctx = lax.axis_index("ctx")
    head = lax.axis_index("head")
    tokens = q_hbm.shape[1]
    groups = k_hbm.shape[2] // HEAD_SIZE
    units = SLIDING_LAYERS * groups
    ext = WINDOW_LENGTH + tokens
    chunk = tokens // head_count
    halo_blocks = WINDOW_LENGTH // ROWS
    blocks = tokens // ROWS
    span = WINDOW_LENGTH + ROWS
    pair = 2 * HEAD_SIZE
    after = lax.rem(ctx + 1, ctx_count)
    before = lax.rem(ctx + ctx_count - 1, ctx_count)
    has_before = ctx > 0
    has_after = ctx < ctx_count - 1

    def place(unit):
        return unit // groups, lax.rem(unit, groups)

    def loads(unit):
        layer, group = place(unit)
        wide = pl.ds(pl.multiple_of(group * pair, pair), pair)
        slim = pl.ds(pl.multiple_of(group * HEAD_SIZE, HEAD_SIZE), HEAD_SIZE)
        return [
            pltpu.make_async_copy(
                k_hbm.at[layer, :, slim], k_ext.at[unit, pl.ds(WINDOW_LENGTH, tokens)], load_sem.at[0, unit]
            ),
            pltpu.make_async_copy(
                v_hbm.at[layer, :, slim], v_ext.at[unit, pl.ds(WINDOW_LENGTH, tokens)], load_sem.at[1, unit]
            ),
            pltpu.make_async_copy(q_hbm.at[layer, :, wide], q_all.at[unit], load_sem.at[2, unit]),
            pltpu.make_async_copy(g_hbm.at[layer, :, wide], g_all.at[unit], load_sem.at[3, unit]),
            pltpu.make_async_copy(o_hbm.at[layer, :, wide], o_all.at[unit], load_sem.at[4, unit]),
        ]

    def rims(unit):
        layer, group = place(unit)
        slim = pl.ds(pl.multiple_of(group * HEAD_SIZE, HEAD_SIZE), HEAD_SIZE)
        last = pl.ds(tokens - WINDOW_LENGTH, WINDOW_LENGTH)
        first = pl.ds(0, WINDOW_LENGTH)
        return [
            pltpu.make_async_remote_copy(
                src_ref=source.at[layer, last, slim],
                dst_ref=target.at[unit, first],
                send_sem=rim_send_sem.at[which, unit],
                recv_sem=rim_recv_sem.at[which, unit],
                device_id=(after, head),
                device_id_type=MESH,
            )
            for which, (source, target) in enumerate(((k_hbm, k_ext), (v_hbm, v_ext)))
        ]

    def backs(unit):
        return [
            pltpu.make_async_remote_copy(
                src_ref=back_send.at[which, unit],
                dst_ref=back_recv.at[which, unit],
                send_sem=back_send_sem.at[which, unit],
                recv_sem=back_recv_sem.at[which, unit],
                device_id=(before, head),
                device_id_type=MESH,
            )
            for which in range(2)
        ]

    def exchange(unit, step, which):
        layer, group = place(unit)
        stage, target, width = (
            (dq_stage, dq_out, pair),
            (dk_stage, dk_out, HEAD_SIZE),
            (dv_stage, dv_out, HEAD_SIZE),
        )[which]
        other = lax.rem(head + step, head_count)
        rows = pl.ds(pl.multiple_of(other * chunk, chunk), chunk)
        columns = pl.ds(pl.multiple_of((head * groups + group) * width, width), width)
        if step == 0:
            return pltpu.make_async_copy(
                stage.at[unit, rows], target.at[layer, :, columns], own_sem.at[which, unit]
            )
        return pltpu.make_async_remote_copy(
            src_ref=stage.at[unit, rows],
            dst_ref=target.at[layer, :, columns],
            send_sem=out_send_sem.at[which, unit, step],
            recv_sem=out_recv_sem.at[which, unit, step],
            device_id=(ctx, other),
            device_id_type=MESH,
        )

    for copy in loads(0):
        copy.start()

    barrier = pltpu.get_barrier_semaphore()
    for step in range(1, head_count):
        pl.semaphore_signal(
            barrier, inc=1, device_id=(ctx, lax.rem(head + step, head_count)), device_id_type=MESH
        )
    for other in (before, after):
        pl.semaphore_signal(barrier, inc=1, device_id=(other, head), device_id_type=MESH)

    down = lax.broadcasted_iota(jnp.int32, (ROWS, ROWS), 0)
    along = lax.broadcasted_iota(jnp.int32, (ROWS, ROWS), 1)
    for layer in range(SLIDING_LAYERS):
        win = win_ref[layer]
        for slot, distance in enumerate(BIASED):
            apart = along - down + ROWS * distance
            seen = (apart >= 0) & (apart < win)
            bias[layer, slot] = jnp.where(seen, 0.0, HIDDEN)

    @pl.when(jnp.logical_not(has_before))
    def _():
        for unit in range(units):
            k_ext[unit, pl.ds(0, WINDOW_LENGTH)] = jnp.zeros((WINDOW_LENGTH, HEAD_SIZE), jnp.bfloat16)
            v_ext[unit, pl.ds(0, WINDOW_LENGTH)] = jnp.zeros((WINDOW_LENGTH, HEAD_SIZE), jnp.bfloat16)

    @pl.when(jnp.logical_not(has_after))
    def _():
        for which in range(2):
            for unit in range(units):
                back_recv[which, unit] = jnp.zeros((WINDOW_LENGTH, HEAD_SIZE), jnp.bfloat16)

    pl.semaphore_wait(barrier, head_count + 1)

    @pl.when(has_after)
    def _():
        for unit in range(units):
            for copy in rims(unit):
                copy.start()

    for unit in range(1, units):
        for copy in loads(unit):
            copy.start()

    def turn(unit, lower, upper):
        def step(index, carry):
            rows = pl.ds(pl.multiple_of(index * ROWS, ROWS), ROWS)
            k_turned[:, rows] = k_ext[unit, rows].astype(jnp.float32).T.astype(jnp.bfloat16)
            return carry

        lax.fori_loop(lower, upper, step, 0)

    def block(unit, index):
        layer, group = place(unit)
        start = pl.multiple_of(index * ROWS, ROWS)
        rows = pl.ds(start, ROWS)

        def stacked(ref):
            both = ref[unit, rows]
            return jnp.concatenate([both[:, :HEAD_SIZE], both[:, HEAD_SIZE:]], 0)

        q_rows = stacked(q_all)
        g_rows = stacked(g_all)
        product = g_rows.astype(jnp.float32) * stacked(o_all).astype(jnp.float32)
        high = product.astype(jnp.bfloat16)
        low = (product - high.astype(jnp.float32)).astype(jnp.bfloat16)
        delta = dot(
            jnp.ones((8, 2 * HEAD_SIZE), jnp.bfloat16), jnp.concatenate([high, low], 1), NT
        )[0:1]
        norms = lse_ref[layer, :, rows]
        lse = jnp.concatenate([norms[0:1], norms[1:2]], 1)
        for other in range(1, groups):
            mine = jnp.concatenate([norms[2 * other : 2 * other + 1], norms[2 * other + 1 : 2 * other + 2]], 1)
            lse = jnp.where(group == other, mine, lse)
        lse = lse * LOG2_E
        pieces = span // ROWS
        per = 3
        for first in range(0, pieces, per):
            keys = pl.ds(pl.multiple_of(start + first * ROWS, ROWS), per * ROWS)
            scores = dot(k_ext[unit, keys], q_rows, NT)
            grad_prob = dot(v_ext[unit, keys], g_rows, NT)
            for n in range(per):
                piece = first + n
                distance = pieces - 1 - piece
                outside = jnp.logical_and(jnp.logical_not(has_before), index + piece < halo_blocks)
                offset = lse + jnp.where(outside, -HIDDEN, 0.0)
                part = slice(n * ROWS, (n + 1) * ROWS)
                power = scores[part] * (SCALE * LOG2_E) - offset
                if distance in BIASED:
                    add = bias[layer, BIASED.index(distance)]
                    power = power + jnp.concatenate([add, add], 1)
                prob = jnp.exp2(power)
                grad_score = prob * (grad_prob[part] - delta)
                target = pl.ds(piece * ROWS, ROWS)
                prob_buf[target] = prob.astype(jnp.bfloat16)
                score_buf[target] = grad_score.astype(jnp.bfloat16)
        window = pl.ds(start, span)
        dv_acc[unit, window] += dot(prob_buf[...], g_rows)
        dk_acc[unit, window] += dot(score_buf[...], q_rows)
        dq = (dot(k_turned[:, window], score_buf[...]) * SCALE).T.astype(jnp.bfloat16)
        dq_stage[unit, rows, pl.ds(0, HEAD_SIZE)] = dq[:ROWS]
        dq_stage[unit, rows, pl.ds(HEAD_SIZE, HEAD_SIZE)] = dq[ROWS:]

    def sweep(unit, lower, upper):
        def step(index, carry):
            block(unit, index)
            return carry

        lax.fori_loop(lower, upper, step, 0)

    def finish(unit):
        @pl.when(has_after)
        def _():
            for copy in backs(unit):
                copy.wait_recv()

        own = tokens - WINDOW_LENGTH
        for which, (acc, stage) in enumerate(((dk_acc, dk_stage), (dv_acc, dv_stage))):
            factor = SCALE if which == 0 else 1.0

            def step(index, carry, acc=acc, stage=stage, which=which, factor=factor):
                rows = pl.ds(pl.multiple_of(index * ROWS, ROWS), ROWS)
                source = pl.ds(pl.multiple_of(index * ROWS + WINDOW_LENGTH + own, ROWS), ROWS)
                total = acc[unit, source] * factor + back_recv[which, unit, rows].astype(jnp.float32)
                stage[unit, pl.ds(pl.multiple_of(index * ROWS + own, ROWS), ROWS)] = total.astype(jnp.bfloat16)
                return carry

            stage[unit, pl.ds(0, own)] = (acc[unit, pl.ds(WINDOW_LENGTH, own)] * factor).astype(jnp.bfloat16)
            lax.fori_loop(0, halo_blocks, step, 0)
        for step in list(range(1, head_count)) + [0]:
            for which in (1, 2):
                exchange(unit, step, which).start()

    def one_unit(unit, carry):
        for copy in loads(unit):
            copy.wait()
        dk_acc[unit] = jnp.zeros((ext, HEAD_SIZE), jnp.float32)
        dv_acc[unit] = jnp.zeros((ext, HEAD_SIZE), jnp.float32)
        turn(unit, halo_blocks, halo_blocks + blocks)
        sweep(unit, halo_blocks, blocks)

        @pl.when(unit > 0)
        def _():
            finish(unit - 1)

        @pl.when(has_before)
        def _():
            for copy in rims(unit):
                copy.wait_recv()

        turn(unit, 0, halo_blocks)
        sweep(unit, 0, halo_blocks)
        for which, (acc, factor) in enumerate(((dk_acc, SCALE), (dv_acc, 1.0))):
            back_send[which, unit] = (acc[unit, pl.ds(0, WINDOW_LENGTH)] * factor).astype(jnp.bfloat16)

        @pl.when(has_before)
        def _():
            for copy in backs(unit):
                copy.start()

        for step in list(range(1, head_count)) + [0]:
            exchange(unit, step, 0).start()
        return carry

    lax.fori_loop(0, units, one_unit, 0)
    finish(units - 1)

    def drain(unit, carry):
        @pl.when(has_after)
        def _():
            for copy in rims(unit):
                copy.wait_send()

        @pl.when(has_before)
        def _():
            for copy in backs(unit):
                copy.wait_send()

        for which in range(3):
            exchange(unit, 0, which).wait()
            for step in range(1, head_count):
                exchange(unit, step, which).wait()
        return carry

    lax.fori_loop(0, units, drain, 0)


def shards(ctx_count, head_count, queries, keys, values, attn_out, grad_out, log_norm, window):
    tokens = queries.shape[1]
    groups = keys.shape[2] // HEAD_SIZE
    units = SLIDING_LAYERS * groups
    ext = WINDOW_LENGTH + tokens
    pair = 2 * HEAD_SIZE
    span = WINDOW_LENGTH + ROWS
    rows_out = tokens // head_count
    low, wide = jnp.bfloat16, jnp.float32
    anywhere = pl.BlockSpec(memory_space=pl.ANY)
    dma = pltpu.SemaphoreType.DMA
    return pl.pallas_call(
        functools.partial(kernel, head_count, ctx_count),
        out_shape=(
            jax.ShapeDtypeStruct((SLIDING_LAYERS, rows_out, queries.shape[2] * head_count), low),
            jax.ShapeDtypeStruct((SLIDING_LAYERS, rows_out, keys.shape[2] * head_count), low),
            jax.ShapeDtypeStruct((SLIDING_LAYERS, rows_out, values.shape[2] * head_count), low),
        ),
        in_specs=[
            pl.BlockSpec(memory_space=pltpu.SMEM),
            pl.BlockSpec(memory_space=pltpu.VMEM),
            anywhere,
            anywhere,
            anywhere,
            anywhere,
            anywhere,
        ],
        out_specs=(anywhere, anywhere, anywhere),
        scratch_shapes=[
            pltpu.VMEM((units, tokens, pair), low),
            pltpu.VMEM((units, tokens, pair), low),
            pltpu.VMEM((units, tokens, pair), low),
            pltpu.VMEM((units, ext, HEAD_SIZE), low),
            pltpu.VMEM((units, ext, HEAD_SIZE), low),
            pltpu.VMEM((HEAD_SIZE, ext), low),
            pltpu.VMEM((SLIDING_LAYERS, len(BIASED), ROWS, ROWS), wide),
            pltpu.VMEM((span, 2 * ROWS), low),
            pltpu.VMEM((span, 2 * ROWS), low),
            pltpu.VMEM((units, ext, HEAD_SIZE), wide),
            pltpu.VMEM((units, ext, HEAD_SIZE), wide),
            pltpu.VMEM((units, tokens, pair), low),
            pltpu.VMEM((units, tokens, HEAD_SIZE), low),
            pltpu.VMEM((units, tokens, HEAD_SIZE), low),
            pltpu.VMEM((2, units, WINDOW_LENGTH, HEAD_SIZE), low),
            pltpu.VMEM((2, units, WINDOW_LENGTH, HEAD_SIZE), low),
            dma((5, units)),
            dma((2, units)),
            dma((2, units)),
            dma((2, units)),
            dma((2, units)),
            dma((3, units, head_count)),
            dma((3, units, head_count)),
            dma((3, units)),
        ],
        compiler_params=pltpu.CompilerParams(
            collective_id=0, has_side_effects=True, vmem_limit_bytes=60 * 2**20
        ),
        name="band_grads",
    )(window, log_norm, queries, keys, values, attn_out, grad_out)


def solution(mesh):
    in_specs = (
        P(None, "ctx", "head"),
        P(None, "ctx", "head"),
        P(None, "ctx", "head"),
        P(None, "ctx", "head"),
        P(None, "ctx", "head"),
        P(None, "head", "ctx"),
        P(),
    )
    out_specs = (
        P(None, ("ctx", "head"), None),
        P(None, ("ctx", "head"), None),
        P(None, ("ctx", "head"), None),
    )
    body = functools.partial(shards, mesh.shape["ctx"], mesh.shape["head"])
    return jax.shard_map(body, mesh=mesh, in_specs=in_specs, out_specs=out_specs, check_vma=False)
```

```python
import functools
import math

import jax
import jax.numpy as jnp
from jax import lax
from jax.experimental import pallas as pl
from jax.experimental.pallas import tpu as pltpu
from jax.sharding import PartitionSpec as P

HEAD_SIZE = 128
WINDOW_LENGTH = 1024
QUERY_PRE = 168
SLIDING_LAYERS = 2
ROWS = 128
SCALE = QUERY_PRE ** (-0.5)
LOG2_E = math.log2(math.e)
HIDDEN = -1e30
MESH = pl.DeviceIdType.MESH
ORDER = ((1, 2), (0, 2), (1, 1), (0, 3), (1, 3), (0, 1), (1, 0))
BIASED = (0, 4, 5, 6, 7, 8)
NT = (((1,), (1,)), ((), ()))
NN = (((1,), (0,)), ((), ()))


def dot(a, b, dims=NN):
    return lax.dot_general(a, b, dims, preferred_element_type=jnp.float32)


def kernel(
    head_count,
    ctx_count,
    win_ref,
    lse_ref,
    q_hbm,
    k_hbm,
    v_hbm,
    o_hbm,
    g_hbm,
    dq_out,
    dk_out,
    dv_out,
    q_all,
    g_all,
    o_all,
    k_ext,
    v_ext,
    k_turned,
    bias,
    prob_buf,
    score_buf,
    dk_acc,
    dv_acc,
    dq_stage,
    dk_stage,
    dv_stage,
    back_send,
    back_recv,
    relay,
    load_sem,
    rim_send_sem,
    rim_recv_sem,
    back_send_sem,
    back_recv_sem,
    out_send_sem,
    out_recv_sem,
    own_sem,
    relay_send_sem,
    relay_recv_sem,
):
    ctx = lax.axis_index("ctx")
    head = lax.axis_index("head")
    tokens = q_hbm.shape[1]
    groups = k_hbm.shape[2] // HEAD_SIZE
    units = SLIDING_LAYERS * groups
    ext = WINDOW_LENGTH + tokens
    chunk = tokens // head_count
    halo_blocks = WINDOW_LENGTH // ROWS
    blocks = tokens // ROWS
    span = WINDOW_LENGTH + ROWS
    pair = 2 * HEAD_SIZE
    after = lax.rem(ctx + 1, ctx_count)
    before = lax.rem(ctx + ctx_count - 1, ctx_count)
    has_before = ctx > 0
    has_after = ctx < ctx_count - 1
    seam = ctx_count // 2
    at_seam = (ctx == seam - 1) | (ctx == seam)
    passes_rim = (ctx < seam - 2) & (lax.rem(ctx, 2) == 1)
    passes_back = (ctx >= seam + 2) & (lax.rem(ctx, 2) == 0)
    rim_unit = (ctx + 1) // 2
    back_unit = (ctx - seam - 2) // 2
    last_unit = units - 1
    to_seam = ctx - (seam - 1)
    lag = 1 - (to_seam * to_seam + ctx_count * ctx_count - 1) // (ctx_count * ctx_count)

    def place(unit):
        return unit // groups, lax.rem(unit, groups)

    def loads(unit):
        layer, group = place(unit)
        wide = pl.ds(pl.multiple_of(group * pair, pair), pair)
        slim = pl.ds(pl.multiple_of(group * HEAD_SIZE, HEAD_SIZE), HEAD_SIZE)
        return [
            pltpu.make_async_copy(
                k_hbm.at[layer, :, slim], k_ext.at[unit, pl.ds(WINDOW_LENGTH, tokens)], load_sem.at[0, unit]
            ),
            pltpu.make_async_copy(
                v_hbm.at[layer, :, slim], v_ext.at[unit, pl.ds(WINDOW_LENGTH, tokens)], load_sem.at[1, unit]
            ),
            pltpu.make_async_copy(q_hbm.at[layer, :, wide], q_all.at[unit], load_sem.at[2, unit]),
            pltpu.make_async_copy(g_hbm.at[layer, :, wide], g_all.at[unit], load_sem.at[3, unit]),
            pltpu.make_async_copy(o_hbm.at[layer, :, wide], o_all.at[unit], load_sem.at[4, unit]),
        ]

    def relay_in(which):
        return pltpu.make_async_remote_copy(
            src_ref=relay.at[which],
            dst_ref=relay.at[which],
            send_sem=relay_send_sem.at[which],
            recv_sem=relay_recv_sem.at[which],
            device_id=(seam, head),
            device_id_type=MESH,
        )

    def rims(unit, relayed=False):
        layer, group = place(unit)
        slim = pl.ds(pl.multiple_of(group * HEAD_SIZE, HEAD_SIZE), HEAD_SIZE)
        last = pl.ds(tokens - WINDOW_LENGTH, WINDOW_LENGTH)
        first = pl.ds(0, WINDOW_LENGTH)
        return [
            pltpu.make_async_remote_copy(
                src_ref=source.at[layer, last, slim],
                dst_ref=relay.at[which] if relayed else target.at[unit, first],
                send_sem=rim_send_sem.at[which, unit],
                recv_sem=relay_recv_sem.at[which] if relayed else rim_recv_sem.at[which, unit],
                device_id=(2 * unit - 1 if relayed else after, head),
                device_id_type=MESH,
            )
            for which, (source, target) in enumerate(((k_hbm, k_ext), (v_hbm, v_ext)))
        ]

    def rims_onward():
        return [
            pltpu.make_async_remote_copy(
                src_ref=relay.at[which],
                dst_ref=target.at[rim_unit, pl.ds(0, WINDOW_LENGTH)],
                send_sem=relay_send_sem.at[which],
                recv_sem=rim_recv_sem.at[which, rim_unit],
                device_id=(seam, head),
                device_id_type=MESH,
            )
            for which, target in enumerate((k_ext, v_ext))
        ]

    def backs_onward():
        return [
            pltpu.make_async_remote_copy(
                src_ref=relay.at[which],
                dst_ref=back_recv.at[which, back_unit],
                send_sem=relay_send_sem.at[which],
                recv_sem=back_recv_sem.at[which, back_unit],
                device_id=(seam - 1, head),
                device_id_type=MESH,
            )
            for which in range(2)
        ]

    def backs(unit, relayed=False):
        return [
            pltpu.make_async_remote_copy(
                src_ref=back_send.at[which, unit],
                dst_ref=relay.at[which] if relayed else back_recv.at[which, unit],
                send_sem=back_send_sem.at[which, unit],
                recv_sem=relay_recv_sem.at[which] if relayed else back_recv_sem.at[which, unit],
                device_id=(seam + 2 + 2 * unit if relayed else before, head),
                device_id_type=MESH,
            )
            for which in range(2)
        ]

    def piece_of(unit, other, which):
        layer, group = place(unit)
        stage, target, width = (
            (dq_stage, dq_out, pair),
            (dk_stage, dk_out, HEAD_SIZE),
            (dv_stage, dv_out, HEAD_SIZE),
        )[which]
        rows = pl.ds(pl.multiple_of(other * chunk, chunk), chunk)
        columns = pl.ds(pl.multiple_of((head * groups + group) * width, width), width)
        return stage.at[unit, rows], target.at[layer, :, columns]

    def keep(unit, which):
        source, target = piece_of(unit, head, which)
        return pltpu.make_async_copy(source, target, own_sem.at[which, unit])

    def give(unit, other, which):
        source, target = piece_of(unit, other, which)
        return pltpu.make_async_remote_copy(
            src_ref=source,
            dst_ref=target,
            send_sem=out_send_sem.at[which, unit, other],
            recv_sem=out_recv_sem.at[which, unit, head],
            device_id=(ctx, other),
            device_id_type=MESH,
        )

    def taken(unit, other, which):
        source, target = piece_of(unit, other, which)
        return pltpu.make_async_remote_copy(
            src_ref=source,
            dst_ref=target,
            send_sem=out_send_sem.at[which, unit, other],
            recv_sem=out_recv_sem.at[which, unit, other],
            device_id=(ctx, other),
            device_id_type=MESH,
        )

    for copy in loads(0):
        copy.start()

    barrier = pltpu.get_barrier_semaphore()
    for step in range(1, head_count):
        pl.semaphore_signal(
            barrier, inc=1, device_id=(ctx, lax.rem(head + step, head_count)), device_id_type=MESH
        )
    for other in (before, after):
        pl.semaphore_signal(barrier, inc=1, device_id=(other, head), device_id_type=MESH)

    relays = [2 * unit - 1 for unit in range(1, units)] + [seam + 2 + 2 * unit for unit in range(last_unit)]

    @pl.when(at_seam)
    def _():
        for other in relays:
            pl.semaphore_signal(barrier, inc=1, device_id=(other, head), device_id_type=MESH)

    @pl.when(passes_rim | passes_back)
    def _():
        for other in (seam - 1, seam):
            pl.semaphore_signal(barrier, inc=1, device_id=(other, head), device_id_type=MESH)

    down = lax.broadcasted_iota(jnp.int32, (ROWS, ROWS), 0)
    along = lax.broadcasted_iota(jnp.int32, (ROWS, ROWS), 1)
    for layer in range(SLIDING_LAYERS):
        win = win_ref[layer]
        for slot, distance in enumerate(BIASED):
            apart = along - down + ROWS * distance
            seen = (apart >= 0) & (apart < win)
            bias[layer, slot] = jnp.where(seen, 0.0, HIDDEN)

    @pl.when(jnp.logical_not(has_before))
    def _():
        for unit in range(units):
            k_ext[unit, pl.ds(0, WINDOW_LENGTH)] = jnp.zeros((WINDOW_LENGTH, HEAD_SIZE), jnp.bfloat16)
            v_ext[unit, pl.ds(0, WINDOW_LENGTH)] = jnp.zeros((WINDOW_LENGTH, HEAD_SIZE), jnp.bfloat16)

    @pl.when(jnp.logical_not(has_after))
    def _():
        for which in range(2):
            for unit in range(units):
                back_recv[which, unit] = jnp.zeros((WINDOW_LENGTH, HEAD_SIZE), jnp.bfloat16)

    passes = passes_rim | passes_back

    @pl.when(at_seam)
    def _():
        pl.semaphore_wait(barrier, head_count + 1 + len(relays))

    @pl.when(passes)
    def _():
        pl.semaphore_wait(barrier, head_count + 3)

    @pl.when(jnp.logical_not(at_seam | passes))
    def _():
        pl.semaphore_wait(barrier, head_count + 1)

    @pl.when(has_after & (ctx != seam - 1))
    def _():
        for unit in range(units):
            for copy in rims(unit):
                copy.start()

    @pl.when(ctx == seam - 1)
    def _():
        for unit in range(units):
            for copy in rims(unit, relayed=unit > 0):
                copy.start()

    for unit in range(1, units):
        for copy in loads(unit):
            copy.start()

    def turn(unit, lower, upper):
        def step(index, carry):
            rows = pl.ds(pl.multiple_of(index * ROWS, ROWS), ROWS)
            k_turned[:, rows] = k_ext[unit, rows].astype(jnp.float32).T.astype(jnp.bfloat16)
            return carry

        lax.fori_loop(lower, upper, step, 0)

    def block(unit, index, slot):
        layer, group = place(unit)
        start = pl.multiple_of(index * ROWS, ROWS)
        rows = pl.ds(start, ROWS)

        def stacked(ref):
            both = ref[unit, rows]
            return jnp.concatenate([both[:, :HEAD_SIZE], both[:, HEAD_SIZE:]], 0)

        q_rows = stacked(q_all)
        g_rows = stacked(g_all)
        product = g_rows.astype(jnp.float32) * stacked(o_all).astype(jnp.float32)
        high = product.astype(jnp.bfloat16)
        low = (product - high.astype(jnp.float32)).astype(jnp.bfloat16)
        delta = dot(
            jnp.ones((8, 2 * HEAD_SIZE), jnp.bfloat16), jnp.concatenate([high, low], 1), NT
        )[0:1]
        norms = lse_ref[layer, :, rows]
        lse = jnp.concatenate([norms[0:1], norms[1:2]], 1)
        for other in range(1, groups):
            mine = jnp.concatenate([norms[2 * other : 2 * other + 1], norms[2 * other + 1 : 2 * other + 2]], 1)
            lse = jnp.where(group == other, mine, lse)
        lse = lse * LOG2_E
        pieces = span // ROWS
        per = 3
        for first in range(0, pieces, per):
            keys = pl.ds(pl.multiple_of(start + first * ROWS, ROWS), per * ROWS)
            scores = dot(k_ext[unit, keys], q_rows, NT)
            grad_prob = dot(v_ext[unit, keys], g_rows, NT)
            for n in range(per):
                piece = first + n
                distance = pieces - 1 - piece
                outside = jnp.logical_and(jnp.logical_not(has_before), index + piece < halo_blocks)
                offset = lse + jnp.where(outside, -HIDDEN, 0.0)
                part = slice(n * ROWS, (n + 1) * ROWS)
                power = scores[part] * (SCALE * LOG2_E) - offset
                if distance in BIASED:
                    add = bias[layer, BIASED.index(distance)]
                    power = power + jnp.concatenate([add, add], 1)
                prob = jnp.exp2(power)
                grad_score = prob * (grad_prob[part] - delta)
                target = pl.ds(piece * ROWS, ROWS)
                prob_buf[slot, target] = prob.astype(jnp.bfloat16)
                score_buf[slot, target] = grad_score.astype(jnp.bfloat16)
        window = pl.ds(start, span)
        dv_acc[unit, window] += dot(prob_buf[slot], g_rows)
        dk_acc[unit, window] += dot(score_buf[slot], q_rows)
        dq = (dot(k_turned[:, window], score_buf[slot]) * SCALE).T.astype(jnp.bfloat16)
        dq_stage[unit, rows, pl.ds(0, HEAD_SIZE)] = dq[:ROWS]
        dq_stage[unit, rows, pl.ds(HEAD_SIZE, HEAD_SIZE)] = dq[ROWS:]

    def moved_head(across, along):
        line = head_count // 2
        return lax.rem(head // line + across, 2) * line + lax.rem(lax.rem(head, line) + along, line)

    def finish(unit):
        @pl.when(has_after)
        def _():
            for copy in backs(unit):
                copy.wait_recv()

        own = tokens - WINDOW_LENGTH
        for which, (acc, stage) in enumerate(((dk_acc, dk_stage), (dv_acc, dv_stage))):
            factor = SCALE if which == 0 else 1.0

            def step(index, carry, acc=acc, stage=stage, which=which, factor=factor):
                rows = pl.ds(pl.multiple_of(index * ROWS, ROWS), ROWS)
                source = pl.ds(pl.multiple_of(index * ROWS + WINDOW_LENGTH + own, ROWS), ROWS)
                total = acc[unit, source] * factor + back_recv[which, unit, rows].astype(jnp.float32)
                stage[unit, pl.ds(pl.multiple_of(index * ROWS + own, ROWS), ROWS)] = total.astype(jnp.bfloat16)
                return carry

            stage[unit, pl.ds(0, own)] = (acc[unit, pl.ds(WINDOW_LENGTH, own)] * factor).astype(jnp.bfloat16)
            lax.fori_loop(0, halo_blocks, step, 0)
        for across, along in ORDER:
            for which in (1, 2):
                give(unit, moved_head(across, along), which).start()
        for which in (1, 2):
            keep(unit, which).start()

    def one_unit(unit, carry):
        for copy in loads(unit):
            copy.wait()
        dk_acc[unit] = jnp.zeros((ext, HEAD_SIZE), jnp.float32)
        dv_acc[unit] = jnp.zeros((ext, HEAD_SIZE), jnp.float32)
        turn(unit, halo_blocks, halo_blocks + blocks)
        later = (unit + units - 1) // units

        def one_group(step, carry):
            apart = step - 3 * later
            moved = (apart * apart + 8) // 9
            group = 3 * (1 - moved) + moved * lax.rem(head + step, 3)

            @pl.when(step == 1 - later)
            def _():
                @pl.when(has_before)
                def _():
                    for copy in rims(unit):
                        copy.wait_recv()

                turn(unit, 0, halo_blocks)

            for n in range(3):
                block(unit, 3 * group + n, n)
            for n in range(2):
                other = 2 * group + n

                @pl.when(other == head)
                def _():
                    keep(unit, 0).start()

                @pl.when(other != head)
                def _(other=other):
                    give(unit, other, 0).start()

            @pl.when(step == 3 - later)
            def _():
                for which, (acc, factor) in enumerate(((dk_acc, SCALE), (dv_acc, 1.0))):
                    back_send[which, unit] = (acc[unit, pl.ds(0, WINDOW_LENGTH)] * factor).astype(jnp.bfloat16)

                @pl.when(has_before & ((ctx != seam) | (unit == last_unit)))
                def _():
                    for copy in backs(unit):
                        copy.start()

                @pl.when((ctx == seam) & (unit < last_unit))
                def _():
                    for copy in backs(unit, relayed=True):
                        copy.start()

            @pl.when((4 * unit + step == rim_unit - 1) & passes_rim)
            def _():
                for which, copy in enumerate(rims_onward()):
                    relay_in(which).wait_recv()
                    copy.start()

            @pl.when((unit == back_unit + 1) & (step == 2) & passes_back)
            def _():
                for which, copy in enumerate(backs_onward()):
                    relay_in(which).wait_recv()
                    copy.start()

            @pl.when((unit > lag) & (step == 1 - lag))
            def _():
                finish(unit - 1 - lag)

            return carry

        lax.fori_loop(0, 4, one_group, 0)
        return carry

    lax.fori_loop(0, units, one_unit, 0)
    @pl.when(lag > 0)
    def _():
        finish(units - 2)

    finish(units - 1)

    @pl.when(passes_rim | passes_back)
    def _():
        for which in range(2):
            relay_in(which).wait_send()

    def drain(unit, carry):
        @pl.when(has_after)
        def _():
            for copy in rims(unit):
                copy.wait_send()

        @pl.when(has_before)
        def _():
            for copy in backs(unit):
                copy.wait_send()

        for which in range(3):
            keep(unit, which).wait()
            for step in range(1, head_count):
                taken(unit, lax.rem(head + step, head_count), which).wait()
        return carry

    lax.fori_loop(0, units, drain, 0)


def shards(ctx_count, head_count, queries, keys, values, attn_out, grad_out, log_norm, window):
    tokens = queries.shape[1]
    groups = keys.shape[2] // HEAD_SIZE
    units = SLIDING_LAYERS * groups
    ext = WINDOW_LENGTH + tokens
    pair = 2 * HEAD_SIZE
    span = WINDOW_LENGTH + ROWS
    rows_out = tokens // head_count
    low, wide = jnp.bfloat16, jnp.float32
    anywhere = pl.BlockSpec(memory_space=pl.ANY)
    dma = pltpu.SemaphoreType.DMA
    return pl.pallas_call(
        functools.partial(kernel, head_count, ctx_count),
        out_shape=(
            pltpu.VMEM((SLIDING_LAYERS, rows_out, queries.shape[2] * head_count), low),
            pltpu.VMEM((SLIDING_LAYERS, rows_out, keys.shape[2] * head_count), low),
            pltpu.VMEM((SLIDING_LAYERS, rows_out, values.shape[2] * head_count), low),
        ),
        in_specs=[
            pl.BlockSpec(memory_space=pltpu.SMEM),
            pl.BlockSpec(memory_space=pltpu.VMEM),
            anywhere,
            anywhere,
            anywhere,
            anywhere,
            anywhere,
        ],
        out_specs=(pl.BlockSpec(memory_space=pltpu.VMEM),) * 3,
        scratch_shapes=[
            pltpu.VMEM((units, tokens, pair), low),
            pltpu.VMEM((units, tokens, pair), low),
            pltpu.VMEM((units, tokens, pair), low),
            pltpu.VMEM((units, ext, HEAD_SIZE), low),
            pltpu.VMEM((units, ext, HEAD_SIZE), low),
            pltpu.VMEM((HEAD_SIZE, ext), low),
            pltpu.VMEM((SLIDING_LAYERS, len(BIASED), ROWS, ROWS), wide),
            pltpu.VMEM((3, span, 2 * ROWS), low),
            pltpu.VMEM((3, span, 2 * ROWS), low),
            pltpu.VMEM((units, ext, HEAD_SIZE), wide),
            pltpu.VMEM((units, ext, HEAD_SIZE), wide),
            pltpu.VMEM((units, tokens, pair), low),
            pltpu.VMEM((units, tokens, HEAD_SIZE), low),
            pltpu.VMEM((units, tokens, HEAD_SIZE), low),
            pltpu.VMEM((2, units, WINDOW_LENGTH, HEAD_SIZE), low),
            pltpu.VMEM((2, units, WINDOW_LENGTH, HEAD_SIZE), low),
            pltpu.VMEM((2, WINDOW_LENGTH, HEAD_SIZE), low),
            dma((5, units)),
            dma((2, units)),
            dma((2, units)),
            dma((2, units)),
            dma((2, units)),
            dma((3, units, head_count)),
            dma((3, units, head_count)),
            dma((3, units)),
            dma((2,)),
            dma((2,)),
        ],
        compiler_params=pltpu.CompilerParams(
            collective_id=0, has_side_effects=True, vmem_limit_bytes=50 * 2**20
        ),
        name="band_grads",
    )(window, log_norm, queries, keys, values, attn_out, grad_out)


def solution(mesh):
    in_specs = (
        P(None, "ctx", "head"),
        P(None, "ctx", "head"),
        P(None, "ctx", "head"),
        P(None, "ctx", "head"),
        P(None, "ctx", "head"),
        P(None, "head", "ctx"),
        P(),
    )
    out_specs = (
        P(None, ("ctx", "head"), None),
        P(None, ("ctx", "head"), None),
        P(None, ("ctx", "head"), None),
    )
    body = functools.partial(shards, mesh.shape["ctx"], mesh.shape["head"])
    return jax.shard_map(body, mesh=mesh, in_specs=in_specs, out_specs=out_specs, check_vma=False)
```

```python
import functools
import math

import jax
import jax.numpy as jnp
from jax import lax
from jax.experimental import pallas as pl
from jax.experimental.pallas import tpu as pltpu
from jax.sharding import PartitionSpec as P

HEAD_SIZE = 128
WINDOW_LENGTH = 1024
QUERY_PRE = 168
SLIDING_LAYERS = 2
ROWS = 128
SCALE = QUERY_PRE ** (-0.5)
LOG2_E = math.log2(math.e)
HIDDEN = -1e30
MESH = pl.DeviceIdType.MESH
ORDER = ((1, 2), (0, 2), (1, 1), (0, 3), (1, 3), (0, 1), (1, 0))
BIASED = (0, 4, 5, 6, 7, 8)
NT = (((1,), (1,)), ((), ()))
NN = (((1,), (0,)), ((), ()))


def dot(a, b, dims=NN):
    return lax.dot_general(a, b, dims, preferred_element_type=jnp.float32)


def kernel(
    head_count,
    ctx_count,
    win_ref,
    lse_ref,
    q_hbm,
    k_hbm,
    v_hbm,
    o_hbm,
    g_hbm,
    dq_out,
    dk_out,
    dv_out,
    q_all,
    g_all,
    o_all,
    k_ext,
    v_ext,
    k_turned,
    bias,
    prob_buf,
    score_buf,
    dk_acc,
    dv_acc,
    dq_stage,
    dk_stage,
    dv_stage,
    back_send,
    back_recv,
    relay,
    load_sem,
    rim_send_sem,
    rim_recv_sem,
    back_send_sem,
    back_recv_sem,
    out_send_sem,
    out_recv_sem,
    own_sem,
    relay_send_sem,
    relay_recv_sem,
):
    ctx = lax.axis_index("ctx")
    head = lax.axis_index("head")
    tokens = q_hbm.shape[1]
    groups = k_hbm.shape[2] // HEAD_SIZE
    units = SLIDING_LAYERS * groups
    ext = WINDOW_LENGTH + tokens
    chunk = tokens // head_count
    halo_blocks = WINDOW_LENGTH // ROWS
    blocks = tokens // ROWS
    span = WINDOW_LENGTH + ROWS
    pair = 2 * HEAD_SIZE
    after = lax.rem(ctx + 1, ctx_count)
    before = lax.rem(ctx + ctx_count - 1, ctx_count)
    has_before = ctx > 0
    has_after = ctx < ctx_count - 1
    seam = ctx_count // 2
    at_seam = (ctx == seam - 1) | (ctx == seam)
    passes_rim = (ctx < seam - 2) & (lax.rem(ctx, 2) == 1)
    passes_back = (ctx >= seam + 2) & (lax.rem(ctx, 2) == 0)
    rim_unit = (ctx + 1) // 2
    back_unit = (ctx - seam - 2) // 2
    last_unit = units - 1
    late = 1 - ((ctx - seam) * (ctx - seam) + ctx_count * ctx_count - 1) // (ctx_count * ctx_count)
    to_seam = ctx - (seam - 1)
    lag = 1 - (to_seam * to_seam + ctx_count * ctx_count - 1) // (ctx_count * ctx_count)

    def place(unit):
        return unit // groups, lax.rem(unit, groups)

    def loads(unit):
        layer, group = place(unit)
        wide = pl.ds(pl.multiple_of(group * pair, pair), pair)
        slim = pl.ds(pl.multiple_of(group * HEAD_SIZE, HEAD_SIZE), HEAD_SIZE)
        return [
            pltpu.make_async_copy(
                k_hbm.at[layer, :, slim], k_ext.at[unit, pl.ds(WINDOW_LENGTH, tokens)], load_sem.at[0, unit]
            ),
            pltpu.make_async_copy(
                v_hbm.at[layer, :, slim], v_ext.at[unit, pl.ds(WINDOW_LENGTH, tokens)], load_sem.at[1, unit]
            ),
            pltpu.make_async_copy(q_hbm.at[layer, :, wide], q_all.at[unit], load_sem.at[2, unit]),
            pltpu.make_async_copy(g_hbm.at[layer, :, wide], g_all.at[unit], load_sem.at[3, unit]),
            pltpu.make_async_copy(o_hbm.at[layer, :, wide], o_all.at[unit], load_sem.at[4, unit]),
        ]

    def relay_in(which):
        return pltpu.make_async_remote_copy(
            src_ref=relay.at[which],
            dst_ref=relay.at[which],
            send_sem=relay_send_sem.at[which],
            recv_sem=relay_recv_sem.at[which],
            device_id=(seam, head),
            device_id_type=MESH,
        )

    def rims(unit, relayed=False):
        layer, group = place(unit)
        slim = pl.ds(pl.multiple_of(group * HEAD_SIZE, HEAD_SIZE), HEAD_SIZE)
        last = pl.ds(tokens - WINDOW_LENGTH, WINDOW_LENGTH)
        first = pl.ds(0, WINDOW_LENGTH)
        return [
            pltpu.make_async_remote_copy(
                src_ref=source.at[layer, last, slim],
                dst_ref=relay.at[which] if relayed else target.at[unit, first],
                send_sem=rim_send_sem.at[which, unit],
                recv_sem=relay_recv_sem.at[which] if relayed else rim_recv_sem.at[which, unit],
                device_id=(2 * unit - 1 if relayed else after, head),
                device_id_type=MESH,
            )
            for which, (source, target) in enumerate(((k_hbm, k_ext), (v_hbm, v_ext)))
        ]

    def rims_onward():
        return [
            pltpu.make_async_remote_copy(
                src_ref=relay.at[which],
                dst_ref=target.at[rim_unit, pl.ds(0, WINDOW_LENGTH)],
                send_sem=relay_send_sem.at[which],
                recv_sem=rim_recv_sem.at[which, rim_unit],
                device_id=(seam, head),
                device_id_type=MESH,
            )
            for which, target in enumerate((k_ext, v_ext))
        ]

    def backs_onward():
        return [
            pltpu.make_async_remote_copy(
                src_ref=relay.at[which],
                dst_ref=back_recv.at[which, back_unit],
                send_sem=relay_send_sem.at[which],
                recv_sem=back_recv_sem.at[which, back_unit],
                device_id=(seam - 1, head),
                device_id_type=MESH,
            )
            for which in range(2)
        ]

    def backs(unit, relayed=False):
        return [
            pltpu.make_async_remote_copy(
                src_ref=back_send.at[which, unit],
                dst_ref=relay.at[which] if relayed else back_recv.at[which, unit],
                send_sem=back_send_sem.at[which, unit],
                recv_sem=relay_recv_sem.at[which] if relayed else back_recv_sem.at[which, unit],
                device_id=(seam + 2 + 2 * unit if relayed else before, head),
                device_id_type=MESH,
            )
            for which in range(2)
        ]

    def piece_of(unit, other, which):
        layer, group = place(unit)
        stage, target, width = (
            (dq_stage, dq_out, pair),
            (dk_stage, dk_out, HEAD_SIZE),
            (dv_stage, dv_out, HEAD_SIZE),
        )[which]
        rows = pl.ds(pl.multiple_of(other * chunk, chunk), chunk)
        columns = pl.ds(pl.multiple_of((head * groups + group) * width, width), width)
        return stage.at[unit, rows], target.at[layer, :, columns]

    def keep(unit, which):
        source, target = piece_of(unit, head, which)
        return pltpu.make_async_copy(source, target, own_sem.at[which, unit])

    def give(unit, other, which):
        source, target = piece_of(unit, other, which)
        return pltpu.make_async_remote_copy(
            src_ref=source,
            dst_ref=target,
            send_sem=out_send_sem.at[which, unit, other],
            recv_sem=out_recv_sem.at[which, unit, head],
            device_id=(ctx, other),
            device_id_type=MESH,
        )

    def taken(unit, other, which):
        source, target = piece_of(unit, other, which)
        return pltpu.make_async_remote_copy(
            src_ref=source,
            dst_ref=target,
            send_sem=out_send_sem.at[which, unit, other],
            recv_sem=out_recv_sem.at[which, unit, other],
            device_id=(ctx, other),
            device_id_type=MESH,
        )

    for copy in loads(0):
        copy.start()

    barrier = pltpu.get_barrier_semaphore()
    for step in range(1, head_count):
        pl.semaphore_signal(
            barrier, inc=1, device_id=(ctx, lax.rem(head + step, head_count)), device_id_type=MESH
        )
    for other in (before, after):
        pl.semaphore_signal(barrier, inc=1, device_id=(other, head), device_id_type=MESH)

    relays = [2 * unit - 1 for unit in range(1, units)] + [seam + 2 + 2 * unit for unit in range(last_unit)]

    @pl.when(at_seam)
    def _():
        for other in relays:
            pl.semaphore_signal(barrier, inc=1, device_id=(other, head), device_id_type=MESH)

    @pl.when(passes_rim | passes_back)
    def _():
        for other in (seam - 1, seam):
            pl.semaphore_signal(barrier, inc=1, device_id=(other, head), device_id_type=MESH)

    down = lax.broadcasted_iota(jnp.int32, (ROWS, ROWS), 0)
    along = lax.broadcasted_iota(jnp.int32, (ROWS, ROWS), 1)
    for layer in range(SLIDING_LAYERS):
        win = win_ref[layer]
        for slot, distance in enumerate(BIASED):
            apart = along - down + ROWS * distance
            seen = (apart >= 0) & (apart < win)
            bias[layer, slot] = jnp.where(seen, 0.0, HIDDEN)

    @pl.when(jnp.logical_not(has_before))
    def _():
        for unit in range(units):
            k_ext[unit, pl.ds(0, WINDOW_LENGTH)] = jnp.zeros((WINDOW_LENGTH, HEAD_SIZE), jnp.bfloat16)
            v_ext[unit, pl.ds(0, WINDOW_LENGTH)] = jnp.zeros((WINDOW_LENGTH, HEAD_SIZE), jnp.bfloat16)

    @pl.when(jnp.logical_not(has_after))
    def _():
        for which in range(2):
            for unit in range(units):
                back_recv[which, unit] = jnp.zeros((WINDOW_LENGTH, HEAD_SIZE), jnp.bfloat16)

    passes = passes_rim | passes_back

    @pl.when(at_seam)
    def _():
        pl.semaphore_wait(barrier, head_count + 1 + len(relays))

    @pl.when(passes)
    def _():
        pl.semaphore_wait(barrier, head_count + 3)

    @pl.when(jnp.logical_not(at_seam | passes))
    def _():
        pl.semaphore_wait(barrier, head_count + 1)

    @pl.when(has_after & (ctx != seam - 1))
    def _():
        for unit in range(units):
            for copy in rims(unit):
                copy.start()

    @pl.when(ctx == seam - 1)
    def _():
        for unit in range(units):
            for copy in rims(unit, relayed=unit > 0):
                copy.start()

    for unit in range(1, units):
        for copy in loads(unit):
            copy.start()

    def turn(unit, lower, upper):
        def step(index, carry):
            rows = pl.ds(pl.multiple_of(index * 4 * ROWS, 4 * ROWS), 4 * ROWS)
            k_turned[:, rows] = k_ext[unit, rows].T
            return carry

        lax.fori_loop(lower // 4, upper // 4, step, 0)

    def block(unit, index, slot):
        layer, group = place(unit)
        start = pl.multiple_of(index * ROWS, ROWS)
        rows = pl.ds(start, ROWS)

        def stacked(ref):
            both = ref[unit, rows]
            return jnp.concatenate([both[:, :HEAD_SIZE], both[:, HEAD_SIZE:]], 0)

        q_rows = stacked(q_all)
        g_rows = stacked(g_all)
        product = g_rows.astype(jnp.float32) * stacked(o_all).astype(jnp.float32)
        high = product.astype(jnp.bfloat16)
        low = (product - high.astype(jnp.float32)).astype(jnp.bfloat16)
        delta = dot(
            jnp.ones((8, 2 * HEAD_SIZE), jnp.bfloat16), jnp.concatenate([high, low], 1), NT
        )[0:1]
        norms = lse_ref[layer, :, rows]
        lse = jnp.concatenate([norms[0:1], norms[1:2]], 1)
        for other in range(1, groups):
            mine = jnp.concatenate([norms[2 * other : 2 * other + 1], norms[2 * other + 1 : 2 * other + 2]], 1)
            lse = jnp.where(group == other, mine, lse)
        lse = lse * LOG2_E
        pieces = span // ROWS
        per = 3
        for first in range(0, pieces, per):
            keys = pl.ds(pl.multiple_of(start + first * ROWS, ROWS), per * ROWS)
            scores = dot(k_ext[unit, keys], q_rows, NT)
            grad_prob = dot(v_ext[unit, keys], g_rows, NT)
            for n in range(per):
                piece = first + n
                distance = pieces - 1 - piece
                outside = jnp.logical_and(jnp.logical_not(has_before), index + piece < halo_blocks)
                offset = lse + jnp.where(outside, -HIDDEN, 0.0)
                part = slice(n * ROWS, (n + 1) * ROWS)
                power = scores[part] * (SCALE * LOG2_E) - offset
                if distance in BIASED:
                    add = bias[layer, BIASED.index(distance)]
                    power = power + jnp.concatenate([add, add], 1)
                prob = jnp.exp2(power)
                grad_score = prob * (grad_prob[part] - delta)
                target = pl.ds(piece * ROWS, ROWS)
                prob_buf[slot, target] = prob.astype(jnp.bfloat16)
                score_buf[slot, target] = grad_score.astype(jnp.bfloat16)
        window = pl.ds(start, span)
        dv_acc[unit, window] += dot(prob_buf[slot], g_rows)
        dk_acc[unit, window] += dot(score_buf[slot], q_rows)
        dq = (dot(k_turned[:, window], score_buf[slot]) * SCALE).T.astype(jnp.bfloat16)
        dq_stage[unit, rows, pl.ds(0, HEAD_SIZE)] = dq[:ROWS]
        dq_stage[unit, rows, pl.ds(HEAD_SIZE, HEAD_SIZE)] = dq[ROWS:]

    def moved_head(across, along):
        line = head_count // 2
        return lax.rem(head // line + across, 2) * line + lax.rem(lax.rem(head, line) + along, line)

    def finish(unit):
        own = tokens - WINDOW_LENGTH
        for which, (acc, stage, factor) in enumerate(((dk_acc, dk_stage, SCALE), (dv_acc, dv_stage, 1.0))):

            def step(index, carry, acc=acc, stage=stage, which=which, factor=factor):
                rows = pl.ds(pl.multiple_of(index * ROWS, ROWS), ROWS)
                source = pl.ds(pl.multiple_of(index * ROWS + WINDOW_LENGTH + own, ROWS), ROWS)
                total = acc[unit, source] * factor + back_recv[which, unit, rows].astype(jnp.float32)
                stage[unit, pl.ds(pl.multiple_of(index * ROWS + own, ROWS), ROWS)] = total.astype(jnp.bfloat16)
                return carry

            stage[unit, pl.ds(0, own)] = (acc[unit, pl.ds(WINDOW_LENGTH, own)] * factor).astype(jnp.bfloat16)

            @pl.when(has_after)
            def _(which=which):
                backs(unit)[which].wait_recv()

            lax.fori_loop(0, halo_blocks, step, 0)
            for across, along in ORDER:
                give(unit, moved_head(across, along), which + 1).start()
            keep(unit, which + 1).start()

    def one_unit(unit, carry):
        for copy in loads(unit):
            copy.wait()
        dk_acc[unit] = jnp.zeros((ext, HEAD_SIZE), jnp.float32)
        dv_acc[unit] = jnp.zeros((ext, HEAD_SIZE), jnp.float32)
        turn(unit, halo_blocks, halo_blocks + blocks)
        later = (unit + units - 1) // units

        def one_group(step, carry):
            apart = step - 3 * later
            moved = (apart * apart + 8) // 9
            group = 3 * (1 - moved) + moved * lax.rem(head + step, 3)

            @pl.when(step == 1 - later)
            def _():
                @pl.when(has_before)
                def _():
                    for copy in rims(unit):
                        copy.wait_recv()

                turn(unit, 0, halo_blocks)

            for n in range(3):
                block(unit, 3 * group + n, n)
            @pl.when(step == 3 - later)
            def _():
                for which, (acc, factor) in enumerate(((dk_acc, SCALE), (dv_acc, 1.0))):
                    back_send[which, unit] = (acc[unit, pl.ds(0, WINDOW_LENGTH)] * factor).astype(jnp.bfloat16)

                    @pl.when(has_before & ((ctx != seam) | (unit == last_unit)))
                    def _(which=which):
                        backs(unit)[which].start()

                    @pl.when((ctx == seam) & (unit < last_unit))
                    def _(which=which):
                        backs(unit, relayed=True)[which].start()

            for n in range(2):
                other = 2 * group + n

                @pl.when(other == head)
                def _():
                    keep(unit, 0).start()

                @pl.when(other != head)
                def _(other=other):
                    give(unit, other, 0).start()

            @pl.when((4 * unit + step == rim_unit - 1) & passes_rim)
            def _():
                for which, copy in enumerate(rims_onward()):
                    relay_in(which).wait_recv()
                    copy.start()

            @pl.when((unit == back_unit + 1) & (step == 2) & passes_back)
            def _():
                for which, copy in enumerate(backs_onward()):
                    relay_in(which).wait_recv()
                    copy.start()

            @pl.when((unit > lag) & (step == 1 - lag + late))
            def _():
                finish(unit - 1 - lag)

            return carry

        lax.fori_loop(0, 4, one_group, 0)
        return carry

    lax.fori_loop(0, units, one_unit, 0)
    @pl.when(lag > 0)
    def _():
        finish(units - 2)

    finish(units - 1)

    @pl.when(passes_rim | passes_back)
    def _():
        for which in range(2):
            relay_in(which).wait_send()

    def drain(unit, carry):
        @pl.when(has_after)
        def _():
            for copy in rims(unit):
                copy.wait_send()

        @pl.when(has_before)
        def _():
            for copy in backs(unit):
                copy.wait_send()

        for which in range(3):
            keep(unit, which).wait()
            for step in range(1, head_count):
                taken(unit, lax.rem(head + step, head_count), which).wait()
        return carry

    lax.fori_loop(0, units, drain, 0)


def place_outputs(*refs):
    count = (len(refs) - 1) // 2
    copies = [
        pltpu.make_async_copy(
            refs[n].at[layer], refs[count + n].at[layer], refs[-1].at[n, layer]
        )
        for n in range(count)
        for layer in range(SLIDING_LAYERS)
    ]
    for copy in copies:
        copy.start()
    for copy in copies:
        copy.wait()


def placed(arrays):
    return pl.pallas_call(
        place_outputs,
        out_shape=tuple(jax.ShapeDtypeStruct(a.shape, a.dtype) for a in arrays),
        in_specs=[pl.BlockSpec(memory_space=pltpu.VMEM)] * len(arrays),
        out_specs=(pl.BlockSpec(memory_space=pl.ANY),) * len(arrays),
        scratch_shapes=[pltpu.SemaphoreType.DMA((len(arrays), SLIDING_LAYERS))],
        compiler_params=pltpu.CompilerParams(vmem_limit_bytes=16 * 2**20),
        name="place_outputs",
    )(*arrays)


def shards(ctx_count, head_count, queries, keys, values, attn_out, grad_out, log_norm, window):
    tokens = queries.shape[1]
    groups = keys.shape[2] // HEAD_SIZE
    units = SLIDING_LAYERS * groups
    ext = WINDOW_LENGTH + tokens
    pair = 2 * HEAD_SIZE
    span = WINDOW_LENGTH + ROWS
    rows_out = tokens // head_count
    low, wide = jnp.bfloat16, jnp.float32
    anywhere = pl.BlockSpec(memory_space=pl.ANY)
    dma = pltpu.SemaphoreType.DMA
    results = pl.pallas_call(
        functools.partial(kernel, head_count, ctx_count),
        out_shape=(
            pltpu.VMEM((SLIDING_LAYERS, rows_out, queries.shape[2] * head_count), low),
            pltpu.VMEM((SLIDING_LAYERS, rows_out, keys.shape[2] * head_count), low),
            pltpu.VMEM((SLIDING_LAYERS, rows_out, values.shape[2] * head_count), low),
        ),
        in_specs=[
            pl.BlockSpec(memory_space=pltpu.SMEM),
            pl.BlockSpec(memory_space=pltpu.VMEM),
            anywhere,
            anywhere,
            anywhere,
            anywhere,
            anywhere,
        ],
        out_specs=(pl.BlockSpec(memory_space=pltpu.VMEM),) * 3,
        scratch_shapes=[
            pltpu.VMEM((units, tokens, pair), low),
            pltpu.VMEM((units, tokens, pair), low),
            pltpu.VMEM((units, tokens, pair), low),
            pltpu.VMEM((units, ext, HEAD_SIZE), low),
            pltpu.VMEM((units, ext, HEAD_SIZE), low),
            pltpu.VMEM((HEAD_SIZE, ext), low),
            pltpu.VMEM((SLIDING_LAYERS, len(BIASED), ROWS, ROWS), wide),
            pltpu.VMEM((3, span, 2 * ROWS), low),
            pltpu.VMEM((3, span, 2 * ROWS), low),
            pltpu.VMEM((units, ext, HEAD_SIZE), wide),
            pltpu.VMEM((units, ext, HEAD_SIZE), wide),
            pltpu.VMEM((units, tokens, pair), low),
            pltpu.VMEM((units, tokens, HEAD_SIZE), low),
            pltpu.VMEM((units, tokens, HEAD_SIZE), low),
            pltpu.VMEM((2, units, WINDOW_LENGTH, HEAD_SIZE), low),
            pltpu.VMEM((2, units, WINDOW_LENGTH, HEAD_SIZE), low),
            pltpu.VMEM((2, WINDOW_LENGTH, HEAD_SIZE), low),
            dma((5, units)),
            dma((2, units)),
            dma((2, units)),
            dma((2, units)),
            dma((2, units)),
            dma((3, units, head_count)),
            dma((3, units, head_count)),
            dma((3, units)),
            dma((2,)),
            dma((2,)),
        ],
        compiler_params=pltpu.CompilerParams(
            collective_id=0, has_side_effects=True, vmem_limit_bytes=50 * 2**20
        ),
        name="band_grads",
    )(window, log_norm, queries, keys, values, attn_out, grad_out)
    return placed(results)


def solution(mesh):
    in_specs = (
        P(None, "ctx", "head"),
        P(None, "ctx", "head"),
        P(None, "ctx", "head"),
        P(None, "ctx", "head"),
        P(None, "ctx", "head"),
        P(None, "head", "ctx"),
        P(),
    )
    out_specs = (
        P(None, ("ctx", "head"), None),
        P(None, ("ctx", "head"), None),
        P(None, ("ctx", "head"), None),
    )
    body = functools.partial(shards, mesh.shape["ctx"], mesh.shape["head"])
    return jax.shard_map(body, mesh=mesh, in_specs=in_specs, out_specs=out_specs, check_vma=False)
```

```python
import functools
import math

import jax
import jax.numpy as jnp
from jax import lax
from jax.experimental import pallas as pl
from jax.experimental.pallas import tpu as pltpu
from jax.sharding import PartitionSpec as P

HEAD_SIZE = 128
WINDOW_LENGTH = 1024
QUERY_PRE = 168
SLIDING_LAYERS = 2
ROWS = 128
SCALE = QUERY_PRE ** (-0.5)
LOG2_E = math.log2(math.e)
HIDDEN = -1e30
MESH = pl.DeviceIdType.MESH
ORDER = ((1, 2), (0, 2), (1, 1), (0, 3), (1, 3), (0, 1), (1, 0))
BIASED = (0, 4, 5, 6, 7, 8)
NT = (((1,), (1,)), ((), ()))
NN = (((1,), (0,)), ((), ()))


def dot(a, b, dims=NN):
    return lax.dot_general(a, b, dims, preferred_element_type=jnp.float32)


def kernel(
    head_count,
    ctx_count,
    win_ref,
    lse_ref,
    q_hbm,
    k_hbm,
    v_hbm,
    o_hbm,
    g_hbm,
    dq_out,
    dk_out,
    dv_out,
    q_all,
    g_all,
    o_all,
    k_ext,
    v_ext,
    k_turned,
    bias,
    prob_buf,
    score_buf,
    dk_acc,
    dv_acc,
    dq_stage,
    dk_stage,
    dv_stage,
    back_send,
    back_recv,
    relay,
    load_sem,
    rim_send_sem,
    rim_recv_sem,
    back_send_sem,
    back_recv_sem,
    out_send_sem,
    out_recv_sem,
    own_sem,
    relay_send_sem,
    relay_recv_sem,
):
    ctx = lax.axis_index("ctx")
    head = lax.axis_index("head")
    tokens = q_hbm.shape[1]
    groups = k_hbm.shape[2] // HEAD_SIZE
    units = SLIDING_LAYERS * groups
    ext = WINDOW_LENGTH + tokens
    chunk = tokens // head_count
    halo_blocks = WINDOW_LENGTH // ROWS
    blocks = tokens // ROWS
    span = WINDOW_LENGTH + ROWS
    pair = 2 * HEAD_SIZE
    after = lax.rem(ctx + 1, ctx_count)
    before = lax.rem(ctx + ctx_count - 1, ctx_count)
    has_before = ctx > 0
    has_after = ctx < ctx_count - 1
    seam = ctx_count // 2
    at_seam = (ctx == seam - 1) | (ctx == seam)
    passes_rim = (ctx < seam - 2) & (lax.rem(ctx, 2) == 1)
    passes_back = (ctx >= seam + 2) & (lax.rem(ctx, 2) == 0)
    rim_unit = (ctx + 1) // 2
    back_unit = (ctx - seam - 2) // 2
    last_unit = units - 1
    late = 1 - ((ctx - seam) * (ctx - seam) + ctx_count * ctx_count - 1) // (ctx_count * ctx_count)
    to_seam = ctx - (seam - 1)
    lag = 1 - (to_seam * to_seam + ctx_count * ctx_count - 1) // (ctx_count * ctx_count)

    def place(unit):
        return unit // groups, lax.rem(unit, groups)

    def loads(unit):
        layer, group = place(unit)
        wide = pl.ds(pl.multiple_of(group * pair, pair), pair)
        slim = pl.ds(pl.multiple_of(group * HEAD_SIZE, HEAD_SIZE), HEAD_SIZE)
        return [
            pltpu.make_async_copy(
                k_hbm.at[layer, :, slim], k_ext.at[unit, pl.ds(WINDOW_LENGTH, tokens)], load_sem.at[0, unit]
            ),
            pltpu.make_async_copy(
                v_hbm.at[layer, :, slim], v_ext.at[unit, pl.ds(WINDOW_LENGTH, tokens)], load_sem.at[1, unit]
            ),
            pltpu.make_async_copy(q_hbm.at[layer, :, wide], q_all.at[unit], load_sem.at[2, unit]),
            pltpu.make_async_copy(g_hbm.at[layer, :, wide], g_all.at[unit], load_sem.at[3, unit]),
            pltpu.make_async_copy(o_hbm.at[layer, :, wide], o_all.at[unit], load_sem.at[4, unit]),
        ]

    def relay_in(which):
        return pltpu.make_async_remote_copy(
            src_ref=relay.at[which],
            dst_ref=relay.at[which],
            send_sem=relay_send_sem.at[which],
            recv_sem=relay_recv_sem.at[which],
            device_id=(seam, head),
            device_id_type=MESH,
        )

    def rims(unit, relayed=False):
        layer, group = place(unit)
        slim = pl.ds(pl.multiple_of(group * HEAD_SIZE, HEAD_SIZE), HEAD_SIZE)
        last = pl.ds(tokens - WINDOW_LENGTH, WINDOW_LENGTH)
        first = pl.ds(0, WINDOW_LENGTH)
        return [
            pltpu.make_async_remote_copy(
                src_ref=source.at[layer, last, slim],
                dst_ref=relay.at[which] if relayed else target.at[unit, first],
                send_sem=rim_send_sem.at[which, unit],
                recv_sem=relay_recv_sem.at[which] if relayed else rim_recv_sem.at[which, unit],
                device_id=(2 * unit - 1 if relayed else after, head),
                device_id_type=MESH,
            )
            for which, (source, target) in enumerate(((k_hbm, k_ext), (v_hbm, v_ext)))
        ]

    def rims_onward():
        return [
            pltpu.make_async_remote_copy(
                src_ref=relay.at[which],
                dst_ref=target.at[rim_unit, pl.ds(0, WINDOW_LENGTH)],
                send_sem=relay_send_sem.at[which],
                recv_sem=rim_recv_sem.at[which, rim_unit],
                device_id=(seam, head),
                device_id_type=MESH,
            )
            for which, target in enumerate((k_ext, v_ext))
        ]

    def backs_onward():
        return [
            pltpu.make_async_remote_copy(
                src_ref=relay.at[which],
                dst_ref=back_recv.at[which, back_unit],
                send_sem=relay_send_sem.at[which],
                recv_sem=back_recv_sem.at[which, back_unit],
                device_id=(seam - 1, head),
                device_id_type=MESH,
            )
            for which in range(2)
        ]

    def backs(unit, relayed=False):
        return [
            pltpu.make_async_remote_copy(
                src_ref=back_send.at[which, unit],
                dst_ref=relay.at[which] if relayed else back_recv.at[which, unit],
                send_sem=back_send_sem.at[which, unit],
                recv_sem=relay_recv_sem.at[which] if relayed else back_recv_sem.at[which, unit],
                device_id=(seam + 2 + 2 * unit if relayed else before, head),
                device_id_type=MESH,
            )
            for which in range(2)
        ]

    def piece_of(unit, other, which):
        layer, group = place(unit)
        stage, target, width = (
            (dq_stage, dq_out, pair),
            (dk_stage, dk_out, HEAD_SIZE),
            (dv_stage, dv_out, HEAD_SIZE),
        )[which]
        rows = pl.ds(pl.multiple_of(other * chunk, chunk), chunk)
        columns = pl.ds(pl.multiple_of((head * groups + group) * width, width), width)
        return stage.at[unit, rows], target.at[layer, :, columns]

    def keep(unit, which):
        source, target = piece_of(unit, head, which)
        return pltpu.make_async_copy(source, target, own_sem.at[which, unit])

    def give(unit, other, which):
        source, target = piece_of(unit, other, which)
        return pltpu.make_async_remote_copy(
            src_ref=source,
            dst_ref=target,
            send_sem=out_send_sem.at[which, unit, other],
            recv_sem=out_recv_sem.at[which, unit, head],
            device_id=(ctx, other),
            device_id_type=MESH,
        )

    def taken(unit, other, which):
        source, target = piece_of(unit, other, which)
        return pltpu.make_async_remote_copy(
            src_ref=source,
            dst_ref=target,
            send_sem=out_send_sem.at[which, unit, other],
            recv_sem=out_recv_sem.at[which, unit, other],
            device_id=(ctx, other),
            device_id_type=MESH,
        )

    for copy in loads(0):
        copy.start()

    barrier = pltpu.get_barrier_semaphore()
    for step in range(1, head_count):
        pl.semaphore_signal(
            barrier, inc=1, device_id=(ctx, lax.rem(head + step, head_count)), device_id_type=MESH
        )
    for other in (before, after):
        pl.semaphore_signal(barrier, inc=1, device_id=(other, head), device_id_type=MESH)

    relays = [2 * unit - 1 for unit in range(1, units)] + [seam + 2 + 2 * unit for unit in range(last_unit)]

    @pl.when(at_seam)
    def _():
        for other in relays:
            pl.semaphore_signal(barrier, inc=1, device_id=(other, head), device_id_type=MESH)

    @pl.when(passes_rim | passes_back)
    def _():
        for other in (seam - 1, seam):
            pl.semaphore_signal(barrier, inc=1, device_id=(other, head), device_id_type=MESH)

    down = lax.broadcasted_iota(jnp.int32, (ROWS, ROWS), 0)
    along = lax.broadcasted_iota(jnp.int32, (ROWS, ROWS), 1)
    for layer in range(SLIDING_LAYERS):
        win = win_ref[layer]
        for slot, distance in enumerate(BIASED):
            apart = along - down + ROWS * distance
            seen = (apart >= 0) & (apart < win)
            bias[layer, slot] = jnp.where(seen, 0.0, HIDDEN)

    @pl.when(jnp.logical_not(has_before))
    def _():
        for unit in range(units):
            k_ext[unit, pl.ds(0, WINDOW_LENGTH)] = jnp.zeros((WINDOW_LENGTH, HEAD_SIZE), jnp.bfloat16)
            v_ext[unit, pl.ds(0, WINDOW_LENGTH)] = jnp.zeros((WINDOW_LENGTH, HEAD_SIZE), jnp.bfloat16)

    @pl.when(jnp.logical_not(has_after))
    def _():
        for which in range(2):
            for unit in range(units):
                back_recv[which, unit] = jnp.zeros((WINDOW_LENGTH, HEAD_SIZE), jnp.bfloat16)

    passes = passes_rim | passes_back

    @pl.when(at_seam)
    def _():
        pl.semaphore_wait(barrier, head_count + 1 + len(relays))

    @pl.when(passes)
    def _():
        pl.semaphore_wait(barrier, head_count + 3)

    @pl.when(jnp.logical_not(at_seam | passes))
    def _():
        pl.semaphore_wait(barrier, head_count + 1)

    @pl.when(has_after & (ctx != seam - 1))
    def _():
        for unit in range(units):
            for copy in rims(unit):
                copy.start()

    @pl.when(ctx == seam - 1)
    def _():
        for unit in range(units):
            for copy in rims(unit, relayed=unit > 0):
                copy.start()

    for unit in range(1, units):
        for copy in loads(unit):
            copy.start()

    def turn(unit, lower, upper):
        def step(index, carry):
            rows = pl.ds(pl.multiple_of(index * 4 * ROWS, 4 * ROWS), 4 * ROWS)
            k_turned[:, rows] = k_ext[unit, rows].T
            return carry

        lax.fori_loop(lower // 4, upper // 4, step, 0)

    def block(unit, index, slot):
        layer, group = place(unit)
        start = pl.multiple_of(index * ROWS, ROWS)
        rows = pl.ds(start, ROWS)

        def stacked(ref):
            both = ref[unit, rows]
            return jnp.concatenate([both[:, :HEAD_SIZE], both[:, HEAD_SIZE:]], 0)

        q_rows = stacked(q_all)
        g_rows = stacked(g_all)
        product = g_rows.astype(jnp.float32) * stacked(o_all).astype(jnp.float32)
        high = product.astype(jnp.bfloat16)
        low = (product - high.astype(jnp.float32)).astype(jnp.bfloat16)
        delta = dot(
            jnp.ones((8, 2 * HEAD_SIZE), jnp.bfloat16), jnp.concatenate([high, low], 1), NT
        )[0:1]
        norms = lse_ref[layer, :, rows]
        lse = jnp.concatenate([norms[0:1], norms[1:2]], 1)
        for other in range(1, groups):
            mine = jnp.concatenate([norms[2 * other : 2 * other + 1], norms[2 * other + 1 : 2 * other + 2]], 1)
            lse = jnp.where(group == other, mine, lse)
        lse = lse * LOG2_E
        pieces = span // ROWS
        per = 3
        for first in range(0, pieces, per):
            keys = pl.ds(pl.multiple_of(start + first * ROWS, ROWS), per * ROWS)
            scores = dot(k_ext[unit, keys], q_rows, NT)
            grad_prob = dot(v_ext[unit, keys], g_rows, NT)
            for n in range(per):
                piece = first + n
                distance = pieces - 1 - piece
                outside = jnp.logical_and(jnp.logical_not(has_before), index + piece < halo_blocks)
                offset = lse + jnp.where(outside, -HIDDEN, 0.0)
                part = slice(n * ROWS, (n + 1) * ROWS)
                power = scores[part] * (SCALE * LOG2_E) - offset
                if distance in BIASED:
                    add = bias[layer, BIASED.index(distance)]
                    power = power + jnp.concatenate([add, add], 1)
                prob = jnp.exp2(power)
                grad_score = prob * (grad_prob[part] - delta)
                target = pl.ds(piece * ROWS, ROWS)
                prob_buf[slot, target] = prob.astype(jnp.bfloat16)
                score_buf[slot, target] = grad_score.astype(jnp.bfloat16)
        window = pl.ds(start, span)
        dv_acc[unit, window] += dot(prob_buf[slot], g_rows)
        dk_acc[unit, window] += dot(score_buf[slot], q_rows)
        dq = (dot(k_turned[:, window], score_buf[slot]) * SCALE).T.astype(jnp.bfloat16)
        dq_stage[unit, rows, pl.ds(0, HEAD_SIZE)] = dq[:ROWS]
        dq_stage[unit, rows, pl.ds(HEAD_SIZE, HEAD_SIZE)] = dq[ROWS:]

    def moved_head(across, along):
        line = head_count // 2
        return lax.rem(head // line + across, 2) * line + lax.rem(lax.rem(head, line) + along, line)

    def finish(unit):
        own = tokens - WINDOW_LENGTH
        for which, (acc, stage, factor) in enumerate(((dk_acc, dk_stage, SCALE), (dv_acc, dv_stage, 1.0))):

            def step(index, carry, acc=acc, stage=stage, which=which, factor=factor):
                rows = pl.ds(pl.multiple_of(index * ROWS, ROWS), ROWS)
                source = pl.ds(pl.multiple_of(index * ROWS + WINDOW_LENGTH + own, ROWS), ROWS)
                total = acc[unit, source] * factor + back_recv[which, unit, rows].astype(jnp.float32)
                stage[unit, pl.ds(pl.multiple_of(index * ROWS + own, ROWS), ROWS)] = total.astype(jnp.bfloat16)
                return carry

            stage[unit, pl.ds(0, own)] = (acc[unit, pl.ds(WINDOW_LENGTH, own)] * factor).astype(jnp.bfloat16)

            @pl.when(has_after)
            def _(which=which):
                backs(unit)[which].wait_recv()

            lax.fori_loop(0, halo_blocks, step, 0, unroll=4)
            for across, along in ORDER:
                give(unit, moved_head(across, along), which + 1).start()
            keep(unit, which + 1).start()

    def one_unit(unit, carry):
        for copy in loads(unit):
            copy.wait()
        dk_acc[unit] = jnp.zeros((ext, HEAD_SIZE), jnp.float32)
        dv_acc[unit] = jnp.zeros((ext, HEAD_SIZE), jnp.float32)
        turn(unit, halo_blocks, halo_blocks + blocks)
        later = (unit + units - 1) // units

        def one_group(step, carry):
            apart = step - 3 * later
            moved = (apart * apart + 8) // 9
            group = 3 * (1 - moved) + moved * lax.rem(head + step, 3)

            @pl.when(step == 1 - later)
            def _():
                @pl.when(has_before)
                def _():
                    for copy in rims(unit):
                        copy.wait_recv()

                turn(unit, 0, halo_blocks)

            for n in range(3):
                block(unit, 3 * group + n, n)
            @pl.when(step == 3 - later)
            def _():
                for which, (acc, factor) in enumerate(((dk_acc, SCALE), (dv_acc, 1.0))):
                    back_send[which, unit] = (acc[unit, pl.ds(0, WINDOW_LENGTH)] * factor).astype(jnp.bfloat16)

                    @pl.when(has_before & ((ctx != seam) | (unit == last_unit)))
                    def _(which=which):
                        backs(unit)[which].start()

                    @pl.when((ctx == seam) & (unit < last_unit))
                    def _(which=which):
                        backs(unit, relayed=True)[which].start()

            for n in range(2):
                other = 2 * group + n

                @pl.when(other == head)
                def _():
                    keep(unit, 0).start()

                @pl.when(other != head)
                def _(other=other):
                    give(unit, other, 0).start()

            @pl.when((4 * unit + step == rim_unit - 1) & passes_rim)
            def _():
                for which, copy in enumerate(rims_onward()):
                    relay_in(which).wait_recv()
                    copy.start()

            @pl.when((unit == back_unit + 1) & (step == 1) & passes_back)
            def _():
                for which, copy in enumerate(backs_onward()):
                    relay_in(which).wait_recv()
                    copy.start()

            @pl.when((unit > lag) & (step == 1 - lag + late))
            def _():
                finish(unit - 1 - lag)

            return carry

        lax.fori_loop(0, 4, one_group, 0)
        return carry

    lax.fori_loop(0, units, one_unit, 0)
    @pl.when(lag > 0)
    def _():
        finish(units - 2)

    finish(units - 1)

    @pl.when(passes_rim | passes_back)
    def _():
        for which in range(2):
            relay_in(which).wait_send()

    def drain(unit, carry):
        @pl.when(has_after)
        def _():
            for copy in rims(unit):
                copy.wait_send()

        @pl.when(has_before)
        def _():
            for copy in backs(unit):
                copy.wait_send()

        for which in range(3):
            keep(unit, which).wait()
            for step in range(1, head_count):
                taken(unit, lax.rem(head + step, head_count), which).wait()
        return carry

    lax.fori_loop(0, units, drain, 0)


def place_outputs(*refs):
    count = (len(refs) - 1) // 2
    copies = [
        pltpu.make_async_copy(
            refs[n].at[layer], refs[count + n].at[layer], refs[-1].at[n, layer]
        )
        for n in range(count)
        for layer in range(SLIDING_LAYERS)
    ]
    for copy in copies:
        copy.start()
    for copy in copies:
        copy.wait()


def placed(arrays):
    return pl.pallas_call(
        place_outputs,
        out_shape=tuple(jax.ShapeDtypeStruct(a.shape, a.dtype) for a in arrays),
        in_specs=[pl.BlockSpec(memory_space=pltpu.VMEM)] * len(arrays),
        out_specs=(pl.BlockSpec(memory_space=pl.ANY),) * len(arrays),
        scratch_shapes=[pltpu.SemaphoreType.DMA((len(arrays), SLIDING_LAYERS))],
        compiler_params=pltpu.CompilerParams(vmem_limit_bytes=16 * 2**20),
        name="place_outputs",
    )(*arrays)


def shards(ctx_count, head_count, queries, keys, values, attn_out, grad_out, log_norm, window):
    tokens = queries.shape[1]
    groups = keys.shape[2] // HEAD_SIZE
    units = SLIDING_LAYERS * groups
    ext = WINDOW_LENGTH + tokens
    pair = 2 * HEAD_SIZE
    span = WINDOW_LENGTH + ROWS
    rows_out = tokens // head_count
    low, wide = jnp.bfloat16, jnp.float32
    anywhere = pl.BlockSpec(memory_space=pl.ANY)
    dma = pltpu.SemaphoreType.DMA
    results = pl.pallas_call(
        functools.partial(kernel, head_count, ctx_count),
        out_shape=(
            pltpu.VMEM((SLIDING_LAYERS, rows_out, queries.shape[2] * head_count), low),
            pltpu.VMEM((SLIDING_LAYERS, rows_out, keys.shape[2] * head_count), low),
            pltpu.VMEM((SLIDING_LAYERS, rows_out, values.shape[2] * head_count), low),
        ),
        in_specs=[
            pl.BlockSpec(memory_space=pltpu.SMEM),
            pl.BlockSpec(memory_space=pltpu.VMEM),
            anywhere,
            anywhere,
            anywhere,
            anywhere,
            anywhere,
        ],
        out_specs=(pl.BlockSpec(memory_space=pltpu.VMEM),) * 3,
        scratch_shapes=[
            pltpu.VMEM((units, tokens, pair), low),
            pltpu.VMEM((units, tokens, pair), low),
            pltpu.VMEM((units, tokens, pair), low),
            pltpu.VMEM((units, ext, HEAD_SIZE), low),
            pltpu.VMEM((units, ext, HEAD_SIZE), low),
            pltpu.VMEM((HEAD_SIZE, ext), low),
            pltpu.VMEM((SLIDING_LAYERS, len(BIASED), ROWS, ROWS), wide),
            pltpu.VMEM((3, span, 2 * ROWS), low),
            pltpu.VMEM((3, span, 2 * ROWS), low),
            pltpu.VMEM((units, ext, HEAD_SIZE), wide),
            pltpu.VMEM((units, ext, HEAD_SIZE), wide),
            pltpu.VMEM((units, tokens, pair), low),
            pltpu.VMEM((units, tokens, HEAD_SIZE), low),
            pltpu.VMEM((units, tokens, HEAD_SIZE), low),
            pltpu.VMEM((2, units, WINDOW_LENGTH, HEAD_SIZE), low),
            pltpu.VMEM((2, units, WINDOW_LENGTH, HEAD_SIZE), low),
            pltpu.VMEM((2, WINDOW_LENGTH, HEAD_SIZE), low),
            dma((5, units)),
            dma((2, units)),
            dma((2, units)),
            dma((2, units)),
            dma((2, units)),
            dma((3, units, head_count)),
            dma((3, units, head_count)),
            dma((3, units)),
            dma((2,)),
            dma((2,)),
        ],
        compiler_params=pltpu.CompilerParams(
            collective_id=0, has_side_effects=True, vmem_limit_bytes=50 * 2**20
        ),
        name="band_grads",
    )(window, log_norm, queries, keys, values, attn_out, grad_out)
    return placed(results)


def solution(mesh):
    in_specs = (
        P(None, "ctx", "head"),
        P(None, "ctx", "head"),
        P(None, "ctx", "head"),
        P(None, "ctx", "head"),
        P(None, "ctx", "head"),
        P(None, "head", "ctx"),
        P(),
    )
    out_specs = (
        P(None, ("ctx", "head"), None),
        P(None, ("ctx", "head"), None),
        P(None, ("ctx", "head"), None),
    )
    body = functools.partial(shards, mesh.shape["ctx"], mesh.shape["head"])
    return jax.shard_map(body, mesh=mesh, in_specs=in_specs, out_specs=out_specs, check_vma=False)
```
